32 devices in a mesh: dp: 8 (over z, core), tensor: 4 (over y, x).
Axes of the slice: x: 2, y: 2, z: 4, core: 2. Of those that a mesh axis runs over, the one named last changes fastest.
Arguments:
- tokens: bfloat16 [8192, 2048], P('dp'), may hold values from -6 to 6
- lengths: int32 [64], P('dp'), may hold values from 1 to 64, 2560 in all
- cotangent: bfloat16 [8192, 2048], P('dp'), may hold values from -6 to 6
- pre_gain: float32 [2048], replicated, may hold values from 0.5 to 1.5
- pre_shift: float32 [2048], replicated, may hold values from -1.5 to 1.5
- qkv_weight: bfloat16 [3, 2048, 2048], P(None, None, 'tensor'), may hold values from -0.125 to 0.125
- qkv_bias: float32 [3, 2048], P(None, 'tensor'), may hold values from -1.5 to 1.5
- mix_gain: float32 [2048], P('tensor'), may hold values from 0.5 to 1.5
- mix_shift: float32 [2048], P('tensor'), may hold values from -1.5 to 1.5
- out_weight: bfloat16 [2048, 2048], P('tensor'), may hold values from -0.125 to 0.125
- out_bias: float32 [2048], replicated, may hold values from -1.5 to 1.5
- ffn_gain: float32 [2048], replicated, may hold values from 0.5 to 1.5
- ffn_shift: float32 [2048], replicated, may hold values from -1.5 to 1.5
- up_weight: bfloat16 [2048, 8192], P(None, 'tensor'), may hold values from -0.125 to 0.125
- up_bias: float32 [8192], P('tensor'), may hold values from -2.5 to 2.5
- hid_gain: float32 [8192], P('tensor'), may hold values from 0.5 to 1.5
- hid_shift: float32 [8192], P('tensor'), may hold values from -1.5 to 1.5
- down_weight: bfloat16 [8192, 2048], P('tensor'), may hold values from -0.0625 to 0.0625
- down_bias: float32 [2048], replicated, may hold values from -1.5 to 1.5
Outputs:
- output: bfloat16 [8192, 2048], P('dp')
- tokens_grad: float32 [8192, 2048], P('dp')
- pre_gain_grad: float32 [2048], replicated
- pre_shift_grad: float32 [2048], replicated
- qkv_weight_grad: float32 [3, 2048, 2048], P(None, 'dp', 'tensor')
- qkv_bias_grad: float32 [3, 2048], P(None, 'tensor')
- mix_gain_grad: float32 [2048], P('tensor')
- mix_shift_grad: float32 [2048], P('tensor')
- out_weight_grad: float32 [2048, 2048], P('tensor', 'dp')
- out_bias_grad: float32 [2048], replicated
- ffn_gain_grad: float32 [2048], replicated
- ffn_shift_grad: float32 [2048], replicated
- up_weight_grad: float32 [2048, 8192], P('dp', 'tensor')
- up_bias_grad: float32 [8192], P('tensor')
- hid_gain_grad: float32 [8192], P('tensor')
- hid_shift_grad: float32 [8192], P('tensor')
- down_weight_grad: float32 [8192, 2048], P('tensor', 'dp')
- down_bias_grad: float32 [2048], replicated
The draws below stay inside these ranges and needn't reach their ends.
Inputs may be any that keep to these rules, and one draw needn't show every extreme that they name: Caption length of each pair; the lengths sum to 2560 and the longest is 64.
All inputs are finite; a program needn't handle non-finite values. No bound on the sum of `lengths` on one device may be relied on, other than what follows from the above.
Results may differ from the reference program's by a relative error of at most 0.013.
Values sent between devices are 32-bit elements; how exact they have to be, the bound alone decides.
No kernel may reach another device: no remote copies, remote signals or barrier semaphores. Data moves between devices by JAX's collectives and lax.ppermute only.
A program may use at most 256 MiB of HBM per device.

```python
import functools
import math
import jax
import jax.numpy as jnp
import numpy as np
from jax import lax

D = 2048
HEADS = 32
HD = 64
FF = 8192
SLOT = 128
IMG = 64
SCALE_BASE = 512
CAP = 64
PAIRS = 64
TOKENS = 8192


def levels(own_key, dims, pieces, smallest, high):
    factor_of, own = 1.0, jax.random.fold_in(own_key, 6)
    for axis_at, parts in pieces:
        heights = jnp.exp(jax.random.uniform(jax.random.fold_in(own, axis_at), (parts,), jnp.float32, smallest / len(pieces), high / len(pieces)))
        factor_of = factor_of * jnp.repeat(heights, dims[axis_at] // parts).reshape([-1 if axis == axis_at else 1 for axis in range(len(dims))])
    return factor_of


def split_up(number_of, total, most, slope):
    loads = [(1 << 20) // math.isqrt(rank ** slope) + 1 for rank in range(2, number_of + 1)]
    rest, counts = total - most - (number_of - 1), [1] * (number_of - 1)
    while rest > 0:
        candidates = [i for i in range(number_of - 1) if counts[i] < most]
        pool, budget = sum([loads[i] for i in candidates]), rest
        for i in candidates:
            extra = min(most - counts[i], max(1, budget * loads[i] // pool), rest)
            counts[i] = counts[i] + extra
            rest = rest - extra
    return np.array([most] + counts)


def uneven_parts(stream_key, number_of, total, reach, skew):
    if number_of == 2:
        one = jax.random.randint(stream_key, (), max(1, total - reach), min(reach, total - 1) + 1)
        return jnp.stack([one, total - one])
    tallies = jnp.asarray(split_up(number_of, total, reach, skew), jnp.int32)
    couples = (number_of - 1) // 2
    giver, receiver = tallies[1:1 + 2 * couples:2], tallies[2:2 + 2 * couples:2]
    room = jnp.minimum(giver - 1, reach - receiver)
    moved = jax.random.randint(jax.random.fold_in(stream_key, 1), (couples,), 0, 1 << 20) % (room + 1)
    tallies = tallies.at[1:1 + 2 * couples:2].set(giver - moved).at[2:2 + 2 * couples:2].set(receiver + moved)
    return tallies[jax.random.permutation(jax.random.fold_in(stream_key, 2), number_of)]


def centred(stream_key, extent, deviation, limit, cuts=(), kind=jnp.bfloat16):
    entries = deviation * jax.random.normal(stream_key, extent, jnp.float32)
    if cuts:
        entries = entries * levels(stream_key, extent, cuts, -0.22, 0.18)
    return jnp.clip(entries, -limit, limit).astype(kind)


def setup_inputs(seed: int = 0) -> dict:
    key_of = jax.random.split(jax.random.key(seed), 20)
    tokens = centred(key_of[0], (TOKENS, D), 1.0, 6.0, ((0, 8),))
    lengths = uneven_parts(key_of[1], PAIRS, PAIRS * CAP * 5 // 8, CAP, 1).astype(jnp.int32)
    cotangent = centred(key_of[2], (TOKENS, D), 1.0, 6.0, ((0, 8),))
    pre_gain = jnp.clip(1.0 + 0.1 * jax.random.normal(key_of[3], (D,), jnp.float32), 0.5, 1.5)
    pre_shift = centred(key_of[4], (D,), 0.3, 1.5, (), jnp.float32)
    qkv_weight = centred(key_of[5], (3, D, D), D ** -0.5, 0.125, ((2, 4),))
    qkv_bias = centred(key_of[6], (3, D), 0.3, 1.5, ((1, 4),), jnp.float32)
    mix_gain = jnp.clip(1.0 + 0.1 * jax.random.normal(key_of[7], (D,), jnp.float32), 0.5, 1.5)
    mix_shift = centred(key_of[8], (D,), 0.3, 1.5, ((0, 4),), jnp.float32)
    out_weight = centred(key_of[9], (D, D), D ** -0.5, 0.125, ((0, 4),))
    out_bias = centred(key_of[10], (D,), 0.3, 1.5, (), jnp.float32)
    ffn_gain = jnp.clip(1.0 + 0.1 * jax.random.normal(key_of[11], (D,), jnp.float32), 0.5, 1.5)
    ffn_shift = centred(key_of[12], (D,), 0.3, 1.5, (), jnp.float32)
    up_weight = centred(key_of[13], (D, FF), D ** -0.5, 0.125, ((1, 4),))
    up_bias = centred(key_of[14], (FF,), 0.5, 2.5, ((0, 4),), jnp.float32)
    hid_gain = jnp.clip(1.0 + 0.1 * jax.random.normal(key_of[15], (FF,), jnp.float32), 0.5, 1.5)
    hid_shift = centred(key_of[16], (FF,), 0.3, 1.5, ((0, 4),), jnp.float32)
    down_weight = centred(key_of[17], (FF, D), FF ** -0.5, 0.0625, ((0, 4),))
    down_bias = centred(key_of[18], (D,), 0.3, 1.5, (), jnp.float32)
    return {"tokens": tokens, "lengths": lengths, "cotangent": cotangent, "pre_gain": pre_gain, "pre_shift": pre_shift, "qkv_weight": qkv_weight, "qkv_bias": qkv_bias, "mix_gain": mix_gain, "mix_shift": mix_shift, "out_weight": out_weight, "out_bias": out_bias, "ffn_gain": ffn_gain, "ffn_shift": ffn_shift, "up_weight": up_weight, "up_bias": up_bias, "hid_gain": hid_gain, "hid_shift": hid_shift, "down_weight": down_weight, "down_bias": down_bias}


@jax.custom_vjp
def low(v):
    return lax.optimization_barrier(v.astype(jnp.bfloat16)).astype(jnp.float32)

@jax.custom_vjp
def low_back(v):
    return v

def low_keep(v):
    return (low(v), None)

def low_pass(kept, grad):
    return (grad,)

def back_keep(v):
    return (v, None)

def back_low(kept, grad):
    return (low(grad),)
low.defvjp(low_keep, low_pass)
low_back.defvjp(back_keep, back_low)
eps = 1e-05
highest = lax.Precision.HIGHEST

def normalize(value, gain, shift):
    mean = lax.optimization_barrier(jnp.mean(value, axis=-1, keepdims=True))
    var = lax.optimization_barrier(jnp.mean(value * value, axis=-1, keepdims=True)) - mean * mean
    return (value - mean) * lax.rsqrt(var + eps) * gain + shift

def tables():
    place = jnp.arange(SLOT, dtype=jnp.float32)
    index = jnp.arange(HD // 2, dtype=jnp.float32)
    theta = 10000.0 ** (-2.0 * index / HD)
    angle = place[:, None] * theta[None, :]
    zeta = (2.0 * index + 0.4 * HD) / (1.4 * HD)
    growth = zeta[None, :] ** ((place[:, None] - SLOT // 2) / SCALE_BASE)
    return (jnp.cos(angle), jnp.sin(angle), growth)

def rotate(value, cosine, sine, factor):
    shape = value.shape
    pairs = value.reshape(shape[:-1] + (shape[-1] // 2, 2))
    even = pairs[..., 0]
    odd = pairs[..., 1]
    cos_b = cosine[:, None, :]
    sin_b = sine[:, None, :]
    fac_b = factor[:, None, :]
    new_even = (even * cos_b - odd * sin_b) * fac_b
    new_odd = (odd * cos_b + even * sin_b) * fac_b
    return jnp.stack([new_even, new_odd], axis=-1).reshape(shape)

def attend(block):
    query, key, value, length = block
    scale = 1.0 / math.sqrt(HD)
    scores = jnp.einsum('gqhd,gkhd->ghqk', query, key, precision=highest) * scale
    scores = low_back(scores)
    place = jnp.arange(SLOT, dtype=jnp.int32)
    causal = (place[None, :] <= place[:, None])[None, None]
    valid = place[None, None, None, :] < (IMG + length)[:, None, None, None]
    scores = jnp.where(causal & valid, scores, -1e+30)
    probs = jax.nn.softmax(scores, axis=-1)
    return jnp.einsum('ghqk,gkhd->gqhd', low(probs), value, precision=highest)

def forward(lengths, tokens, pre_gain, pre_shift, qkv_weight, qkv_bias, mix_gain, mix_shift, out_weight, out_bias, ffn_gain, ffn_shift, up_weight, up_bias, hid_gain, hid_shift, down_weight, down_bias):
    cosine, sine, growth = tables()
    first = low(normalize(tokens, pre_gain, pre_shift))
    proj = jnp.einsum('td,cde->cte', first, qkv_weight, precision=highest) + qkv_bias[:, None, :]
    proj = low_back(proj)
    shaped = proj.reshape(3, PAIRS, SLOT, HEADS, HD)
    query = low(rotate(shaped[0], cosine, sine, growth))
    key = low(rotate(shaped[1], cosine, sine, 1.0 / growth))
    value = low(shaped[2])
    group = math.gcd(PAIRS, max(1, 4096 // SLOT))
    count = PAIRS // group

    def split(v):
        return v.reshape((count, group) + v.shape[1:])
    mixed = lax.map(jax.checkpoint(attend), (split(query), split(key), split(value), split(lengths)))
    mixed = low_back(mixed.reshape(TOKENS, D))
    mix_low = low(normalize(mixed, mix_gain, mix_shift))
    branch = low_back(jnp.dot(mix_low, out_weight, precision=highest, preferred_element_type=jnp.float32))
    middle = tokens + branch + out_bias
    second = low(normalize(middle, ffn_gain, ffn_shift))
    hidden = low_back(jnp.dot(second, up_weight, precision=highest, preferred_element_type=jnp.float32) + up_bias)
    active = jax.nn.gelu(hidden, approximate=False)
    hid_low = low(normalize(active, hid_gain, hid_shift))
    result = low_back(jnp.dot(hid_low, down_weight, precision=highest, preferred_element_type=jnp.float32))
    return middle + result + down_bias

def reference(tokens, lengths, cotangent, pre_gain, pre_shift, qkv_weight, qkv_bias, mix_gain, mix_shift, out_weight, out_bias, ffn_gain, ffn_shift, up_weight, up_bias, hid_gain, hid_shift, down_weight, down_bias):
    params = [tokens, pre_gain, pre_shift, qkv_weight, qkv_bias, mix_gain, mix_shift, out_weight, out_bias, ffn_gain, ffn_shift, up_weight, up_bias, hid_gain, hid_shift, down_weight, down_bias]
    params = [p.astype(jnp.float32) for p in params]
    final, pull = jax.vjp(functools.partial(forward, lengths), *params)
    grads = pull(cotangent.astype(jnp.float32))
    return (final.astype(jnp.bfloat16), grads[0], grads[1], grads[2], grads[3], grads[4], grads[5], grads[6], grads[7], grads[8], grads[9], grads[10], grads[11], grads[12], grads[13], grads[14], grads[15], grads[16])
```

```python
import functools
import math

import jax
import jax.numpy as jnp
import numpy as np
from jax import lax
from jax.experimental import pallas as pl
from jax.experimental.pallas import tpu as pltpu
from jax.sharding import PartitionSpec as P

D = 2048
HD = 64
FF = 8192
SLOT = 128
IMG = 64
SCALE_BASE = 512
LANES = 128

eps = 1e-05
root_half = 0.7071067811865476
inv_root_two_pi = 0.3989422804014327
masked_score = -1e30
scale = 1.0 / math.sqrt(HD)
bf16 = jnp.bfloat16
f32 = jnp.float32


def rounded(value):
    return value.astype(bf16)


def tables():
    place = np.arange(SLOT, dtype=np.float64)[:, None]
    index = (np.arange(LANES) % HD) // 2
    theta = 10000.0 ** (-2.0 * index / HD)
    angle = place * theta[None, :]
    zeta = (2.0 * index + 0.4 * HD) / (1.4 * HD)
    growth = zeta[None, :] ** ((place - SLOT // 2) / SCALE_BASE)
    sign = np.where(np.arange(LANES) % 2 == 0, -1.0, 1.0)[None, :]
    cosine, sine = np.cos(angle), np.sin(angle) * sign
    return np.stack(
        [cosine * growth, sine * growth, cosine / growth, sine / growth]
    ).astype(np.float32)


def norm_kernel(t_ref, x_ref, gain_ref, shift_ref, o_ref):
    value = x_ref[...].astype(f32)
    mean = jnp.mean(value, axis=-1, keepdims=True)
    var = jnp.mean(value * value, axis=-1, keepdims=True) - mean * mean
    hat = (value - mean) * lax.rsqrt(var + eps)
    o_ref[...] = rounded(hat * gain_ref[...] + shift_ref[...])


def pre_norm(tensor_at, tokens, gain, shift, n, chunk):
    rows = n * SLOT
    return pl.pallas_call(
        norm_kernel,
        out_shape=jax.ShapeDtypeStruct((rows, D), bf16),
        grid_spec=pltpu.PrefetchScalarGridSpec(
            num_scalar_prefetch=1,
            grid=(n,),
            in_specs=[
                pl.BlockSpec((SLOT, D), lambda p, t: (chunk * n + lax.bitwise_xor(p, t[0]), 0)),
                pl.BlockSpec((1, D), lambda p, t: (0, 0)),
                pl.BlockSpec((1, D), lambda p, t: (0, 0)),
            ],
            out_specs=pl.BlockSpec((SLOT, D), lambda p, t: (p, 0)),
        ),
        cost_estimate=pl.CostEstimate(
            flops=8 * rows * D, bytes_accessed=4 * rows * D, transcendentals=0
        ),
        name="pre_norm",
    )(tensor_at, tokens, gain.reshape(1, D), shift.reshape(1, D))


def copy_kernel(t_ref, x_ref, o_ref):
    o_ref[...] = x_ref[...]


def permuted(tensor_at, value, n):
    rows = value.shape[0]
    return pl.pallas_call(
        copy_kernel,
        out_shape=jax.ShapeDtypeStruct(value.shape, value.dtype),
        grid_spec=pltpu.PrefetchScalarGridSpec(
            num_scalar_prefetch=1,
            grid=(rows // SLOT,),
            in_specs=[
                pl.BlockSpec((SLOT, D), lambda i, t: (lax.bitwise_xor(i, t[0]), 0)),
            ],
            out_specs=pl.BlockSpec((SLOT, D), lambda i, t: (i, 0)),
        ),
        cost_estimate=pl.CostEstimate(flops=0, bytes_accessed=4 * rows * D, transcendentals=0),
        name="reorder",
    )(tensor_at, value)


def partner(value, even):
    return jnp.where(
        even, pltpu.roll(value, LANES - 1, axis=1), pltpu.roll(value, 1, axis=1)
    )


def two_heads(value, low_half):
    zero = jnp.zeros_like(value)
    return jnp.concatenate([jnp.where(low_half, value, zero), jnp.where(low_half, zero, value)], 0)


def contract(left, right, dims):
    return lax.dot_general(left, right, (dims, ((), ())), preferred_element_type=f32)


def softmax_two(query, keys, allowed):
    scores = contract(query, keys, ((1,), (1,)))
    halves = []
    for head in range(2):
        part = jnp.where(allowed, scores[:, head * SLOT : (head + 1) * SLOT], masked_score)
        top = jnp.max(part, axis=-1, keepdims=True)
        expd = jnp.exp(part - top)
        halves.append(expd * (1.0 / jnp.sum(expd, axis=-1, keepdims=True)))
    return halves


def masks(length):
    lane = lax.broadcasted_iota(jnp.int32, (SLOT, LANES), 1)
    row = lax.broadcasted_iota(jnp.int32, (SLOT, LANES), 0)
    allowed = (lane <= row) & (lane < IMG + length)
    return lane % 2 == 0, lane < HD, allowed


def attend_kernel(n, chunk, t_ref, len_ref, proj_ref, tab_ref, qkv_ref, mixed_ref, stat_ref):
    p = pl.program_id(0)
    length = len_ref[chunk * n + lax.bitwise_xor(p, t_ref[0])]
    even, low_half, allowed = masks(length)
    width = proj_ref.shape[2]
    total = jnp.zeros((SLOT, 1), f32)
    squares = jnp.zeros((SLOT, 1), f32)
    for at in range(0, width, LANES):
        cols = slice(at, at + LANES)
        q_raw = proj_ref[0, :, cols]
        k_raw = proj_ref[1, :, cols]
        query = rounded(q_raw * tab_ref[0] + partner(q_raw, even) * tab_ref[1]) * bf16(scale)
        key = rounded(k_raw * tab_ref[2] + partner(k_raw, even) * tab_ref[3])
        value = rounded(proj_ref[2, :, cols])
        qkv_ref[0, :, cols] = query
        qkv_ref[1, :, cols] = key
        qkv_ref[2, :, cols] = value
        probs = jnp.concatenate(
            [rounded(v) for v in softmax_two(query, two_heads(key, low_half), allowed)], 1
        )
        mixed = contract(probs, two_heads(value, low_half), ((1,), (0,)))
        mixed_ref[:, cols] = mixed
        total = total + jnp.sum(mixed, axis=-1, keepdims=True)
        squares = squares + jnp.sum(mixed * mixed, axis=-1, keepdims=True)
    lane = lax.broadcasted_iota(jnp.int32, (SLOT, LANES), 1)
    both = jnp.where(lane == 0, total, jnp.where(lane == 1, squares, 0.0))
    stat_ref[...] = both.T[:8]


def attend(tensor_at, lengths, proj, tabs, n, chunk):
    rows, width = proj.shape[1:]
    heads = width // HD
    return pl.pallas_call(
        functools.partial(attend_kernel, n, chunk),
        out_shape=(
            jax.ShapeDtypeStruct((3, rows, width), bf16),
            jax.ShapeDtypeStruct((rows, width), f32),
            jax.ShapeDtypeStruct((8, rows), f32),
        ),
        grid_spec=pltpu.PrefetchScalarGridSpec(
            num_scalar_prefetch=2,
            grid=(n,),
            in_specs=[
                pl.BlockSpec((3, SLOT, width), lambda p, t, l: (0, p, 0)),
                pl.BlockSpec((4, SLOT, LANES), lambda p, t, l: (0, 0, 0)),
            ],
            out_specs=[
                pl.BlockSpec((3, SLOT, width), lambda p, t, l: (0, p, 0)),
                pl.BlockSpec((SLOT, width), lambda p, t, l: (p, 0)),
                pl.BlockSpec((8, SLOT), lambda p, t, l: (0, p)),
            ],
        ),
        cost_estimate=pl.CostEstimate(
            flops=8 * rows * SLOT * width,
            bytes_accessed=22 * rows * width,
            transcendentals=rows * SLOT * heads,
        ),
        name="attend",
    )(tensor_at, lengths, proj, tabs)


def attend_back_kernel(n, chunk, t_ref, len_ref, qkv_ref, grad_ref, tab_ref, out_ref):
    p = pl.program_id(0)
    length = len_ref[chunk * n + lax.bitwise_xor(p, t_ref[0])]
    even, low_half, allowed = masks(length)
    width = grad_ref.shape[1]
    for at in range(0, width, LANES):
        cols = slice(at, at + LANES)
        query = qkv_ref[0, :, cols]
        key = qkv_ref[1, :, cols]
        value = qkv_ref[2, :, cols]
        grad = grad_ref[:, cols]
        keys = two_heads(key, low_half)
        probs = softmax_two(query, keys, allowed)
        prob_grads = contract(grad, two_heads(value, low_half), ((1,), (1,)))
        score_grads = []
        for head in range(2):
            own = prob_grads[:, head * SLOT : (head + 1) * SLOT]
            carried = jnp.sum(probs[head] * own, axis=-1, keepdims=True)
            score_grads.append(rounded(probs[head] * (own - carried)))
        score_grad = jnp.concatenate(score_grads, 1)
        prob_low = jnp.concatenate([rounded(v) for v in probs], 1)
        query_grad = contract(score_grad, keys, ((1,), (0,))) * scale
        key_both = contract(score_grad, query, ((0,), (0,)))
        key_grad = jnp.where(low_half, key_both[:SLOT], key_both[SLOT:])
        value_both = contract(prob_low, grad, ((0,), (0,)))
        value_grad = jnp.where(low_half, value_both[:SLOT], value_both[SLOT:])
        out_ref[0, :, cols] = rounded(
            query_grad * tab_ref[0] - partner(query_grad, even) * tab_ref[1]
        )
        out_ref[1, :, cols] = rounded(
            key_grad * tab_ref[2] - partner(key_grad, even) * tab_ref[3]
        )
        out_ref[2, :, cols] = rounded(value_grad)


def attend_back(tensor_at, lengths, qkv, grad, tabs, n, chunk):
    rows, width = grad.shape
    heads = width // HD
    return pl.pallas_call(
        functools.partial(attend_back_kernel, n, chunk),
        out_shape=jax.ShapeDtypeStruct((3, rows, width), bf16),
        grid_spec=pltpu.PrefetchScalarGridSpec(
            num_scalar_prefetch=2,
            grid=(n,),
            in_specs=[
                pl.BlockSpec((3, SLOT, width), lambda p, t, l: (0, p, 0)),
                pl.BlockSpec((SLOT, width), lambda p, t, l: (p, 0)),
                pl.BlockSpec((4, SLOT, LANES), lambda p, t, l: (0, 0, 0)),
            ],
            out_specs=pl.BlockSpec((3, SLOT, width), lambda p, t, l: (0, p, 0)),
        ),
        cost_estimate=pl.CostEstimate(
            flops=20 * rows * SLOT * width,
            bytes_accessed=14 * rows * width,
            transcendentals=rows * SLOT * heads,
        ),
        name="attend_back",
    )(tensor_at, lengths, qkv, grad, tabs)


def gather_kernel(layout, t_ref, *refs):
    out_ref = refs[-1]
    at = 0
    for place, parts in enumerate(layout):
        where = place if t_ref is None else lax.bitwise_xor(place, t_ref[0])
        left = 0
        for _ in range(parts):
            part = refs[at][...]
            out_ref[where, :, left : left + part.shape[1]] = part.astype(out_ref.dtype)
            left += part.shape[1]
            at += 1


def assembled(blocks):
    n = len(blocks)
    flat = [part for parts in blocks for part in parts]
    tile = 32
    out = pl.pallas_call(
        functools.partial(gather_kernel, [len(parts) for parts in blocks], None),
        out_shape=jax.ShapeDtypeStruct((n, SLOT, D), bf16),
        grid=(SLOT // tile,),
        in_specs=[pl.BlockSpec((tile, part.shape[1]), lambda i: (i, 0)) for part in flat],
        out_specs=pl.BlockSpec((n, tile, D), lambda i: (0, i, 0)),
        cost_estimate=pl.CostEstimate(
            flops=n * SLOT * D, bytes_accessed=6 * n * SLOT * D, transcendentals=0
        ),
        name="assemble",
    )(*flat)
    return out.reshape(n * SLOT, D)


def placed(tensor_at, blocks, chunk, chunks, dtype, before):
    n = len(blocks)
    flat = [part for parts in blocks for part in parts]
    tile = 32
    layout = [len(parts) for parts in blocks]
    extra = [] if before is None else [before]

    def kernel(t_ref, *refs):
        gather_kernel(layout, t_ref, *refs[: len(flat)], refs[-1])

    return pl.pallas_call(
        kernel,
        out_shape=jax.ShapeDtypeStruct((chunks * n, SLOT, D), dtype),
        grid_spec=pltpu.PrefetchScalarGridSpec(
            num_scalar_prefetch=1,
            grid=(SLOT // tile,),
            in_specs=[pl.BlockSpec((tile, part.shape[1]), lambda i, t: (i, 0)) for part in flat]
            + [pl.BlockSpec(memory_space=pl.ANY)] * len(extra),
            out_specs=pl.BlockSpec((n, tile, D), lambda i, t: (chunk, i, 0)),
        ),
        input_output_aliases={1 + len(flat): 0} if extra else {},
        cost_estimate=pl.CostEstimate(
            flops=n * SLOT * D, bytes_accessed=8 * n * SLOT * D, transcendentals=0
        ),
        name="place",
    )(tensor_at, *flat, *extra)


class Links:
    def __init__(self, n, dp):
        self.n, self.dp = n, dp
        self.last = ()

    def swap(self, value, mask, axis="tensor"):
        size = self.n if axis == "tensor" else self.dp
        return lax.ppermute(value, axis, [(i, i ^ mask) for i in range(size)])

    def bits(self, size):
        return [1 << b for b in range(size.bit_length() - 1)]

    def then(self, *values):
        flat, tree = jax.tree.flatten(values)
        flat = lax.optimization_barrier(tuple(flat) + self.last)[: len(flat)]
        values = jax.tree.unflatten(tree, flat)
        return values[0] if len(values) == 1 else values

    def mark(self, *values):
        self.last = tuple(jax.tree.leaves(values))

    def exchange(self, value):
        return [value] + [self.swap(value, mask) for mask in range(1, self.n)]

    def summed(self, held):
        ordered = []
        for mask, value in enumerate(held):
            blocks = [value[:, (p ^ mask) * SLOT : ((p ^ mask) + 1) * SLOT] for p in range(self.n)]
            ordered.append(jnp.concatenate(blocks, 1) if mask else value)
        while len(ordered) > 1:
            ordered = [ordered[i] + ordered[i + 1] for i in range(0, len(ordered), 2)]
        return ordered[0]

    def spread(self, value, axis):
        for mask in self.bits(self.n if axis == "tensor" else self.dp):
            value = value + self.swap(value, mask, axis)
        return value

    def halves(self):
        order = self.bits(self.n)
        if self.n == 4:
            return [(0, D // 2, order), (D // 2, D, order[::-1])]
        return [(0, D, order)]


class Scatter:
    def __init__(self, links, parts):
        self.links, self.at = links, 0
        self.held = [
            {p: [full[p * SLOT : (p + 1) * SLOT]] for p in range(links.n)} for full in parts
        ]
        self.send()

    def send(self):
        self.came, sents = [], []
        for held, (_, _, order) in zip(self.held, self.links.halves()):
            mask = order[self.at]
            away = [p for p in sorted(held) if p & mask]
            sent = [functools.reduce(jnp.add, held.pop(p)) for p in away]
            sent = sent[0] if len(sent) == 1 else jnp.concatenate(sent, 0)
            sents.append(sent)
            self.came.append((away, mask, self.links.swap(sent, mask)))
        self.links.mark(sents)

    def take(self):
        values = self.links.then([came for _, _, came in self.came])
        for held, (away, mask, _), came in zip(self.held, self.came, values):
            for i, p in enumerate(away):
                held[p ^ mask].append(came[i * SLOT : (i + 1) * SLOT])
        self.at += 1

    def step(self):
        while self.at + 1 < len(self.links.halves()[0][2]):
            self.take()
            self.send()

    def finish(self):
        self.take()
        result = [functools.reduce(jnp.add, held[0]) for held in self.held]
        return result[0] if len(result) == 1 else jnp.concatenate(result, 1)


class Gather:
    def __init__(self, links, own):
        self.links, self.own = links, own
        links.mark(own)
        if links.n == 4:
            self.one, self.two = links.swap(own, 1), links.swap(own, 2)

    def step(self):
        if self.links.n == 4:
            one, two = self.links.then(self.one, self.two)
            left, right = two[:, : D // 2], one[:, D // 2 :]
            self.links.mark(left, right)
            self.three = [self.links.swap(left, 1), self.links.swap(right, 2)]

    def result(self):
        if self.links.n == 4:
            three = self.links.then(self.three)
            return [[self.own], [self.one], [self.two], three]
        held = {0: self.own}
        for mask in self.links.bits(self.links.n):
            held.update({p | mask: self.links.swap(v, mask) for p, v in held.items()})
        return [[held[p]] for p in range(self.links.n)]


def local_norm(value):
    mean = jnp.mean(value, axis=-1, keepdims=True)
    var = jnp.mean(value * value, axis=-1, keepdims=True) - mean * mean
    inverse = lax.rsqrt(var + eps)
    return ((value - mean) * inverse, inverse)


def local_back(grad, hat, gain, inverse):
    scaled = grad * gain
    return inverse * (
        scaled
        - jnp.mean(scaled, axis=-1, keepdims=True)
        - hat * jnp.mean(scaled * hat, axis=-1, keepdims=True)
    )


def matmul(left, right):
    return jnp.dot(left, right, preferred_element_type=f32)


def joined(pieces):
    if len(pieces) == 1:
        return pieces[0]
    return jnp.concatenate(lax.optimization_barrier(tuple(pieces)), -2)


def make_body(n, dp):
    links = Links(n, dp)

    def body(
        tokens,
        lengths,
        cotangent,
        pre_gain,
        pre_shift,
        qkv_weight,
        qkv_bias,
        mix_gain,
        mix_shift,
        out_weight,
        out_bias,
        ffn_gain,
        ffn_shift,
        up_weight,
        up_bias,
        hid_gain,
        hid_shift,
        down_weight,
        down_bias,
    ):
        at = lax.axis_index("tensor").astype(jnp.int32)
        tensor_at = at.reshape(1)
        tabs = jnp.asarray(tables())
        rows = n * SLOT
        chunks = tokens.shape[0] // rows
        each = range(chunks)

        def own_rows(value, c):
            return lax.dynamic_slice_in_dim(value, (c * n + at) * SLOT, SLOT, 0).astype(f32)

        def columns(weight):
            return [weight[:, a:b] for a, b, _ in links.halves()]

        first, qkv, mixed, stats = [], [], [], []
        for c in each:
            first.append(pre_norm(tensor_at, tokens, pre_gain, pre_shift, n, c))
            proj = (
                jnp.einsum("td,cde->cte", first[c], qkv_weight, preferred_element_type=f32)
                + qkv_bias[:, None, :]
            )
            held, mix, stat = attend(tensor_at, lengths, proj, tabs, n, c)
            qkv.append(held)
            mixed.append(mix)
            stats.append(links.exchange(stat))
        links.mark(mixed[-1])
        mix_low, mix_hat, mix_inv, branch = [], [], [], []
        for c in each:
            stat = links.summed(links.then(stats[c]))
            mean = stat[0] / D
            inverse = lax.rsqrt(stat[1] / D - mean * mean + eps)
            hat = (mixed[c] - mean[:, None]) * inverse[:, None]
            low = rounded(hat * mix_gain + mix_shift)
            mix_hat.append(hat)
            mix_inv.append(inverse)
            mix_low.append(low)
            branch.append(Scatter(links, [matmul(low, w) for w in columns(out_weight)]))
        cot = permuted(tensor_at, links.then(cotangent), n)
        hid_back = []
        for c in each:
            back = jnp.einsum(
                "td,fd->tf", cot[c * rows : (c + 1) * rows], down_weight, preferred_element_type=f32
            )
            links.mark(back)
            hid_back.append(back)
            branch[c].step()

        middle, ffn_hat, ffn_inv, second = [], [], [], []
        for c in each:
            own = own_rows(tokens, c) + branch[c].finish() + out_bias
            hat, inverse = local_norm(own)
            middle.append(own)
            ffn_hat.append(hat)
            ffn_inv.append(inverse)
            second.append(Gather(links, hat * ffn_gain + ffn_shift))
        for c in each:
            second[c].step()
        hidden, active, scaled, erf, sums = [], [], [], [], []
        for c in each:
            second[c] = assembled(second[c].result())
            hidden.append(matmul(second[c], up_weight) + up_bias)
            erf.append(lax.erf(hidden[c] * root_half))
            active.append(hidden[c] * (0.5 * (1.0 + erf[c])))
            scaled.append(hid_back[c] * hid_gain)
            own = jnp.stack(
                [
                    jnp.sum(active[c], 1),
                    jnp.sum(active[c] * active[c], 1),
                    jnp.sum(scaled[c], 1),
                    jnp.sum(scaled[c] * active[c], 1),
                ]
            )
            links.mark(own)
            sums.append(links.exchange(own))
        hid_low, hidden_grad, second_grad = [], [], []
        hid_gain_grad, hid_shift_grad, up_bias_grad = 0.0, 0.0, 0.0
        for c in each:
            own = links.summed(links.then(sums[c]))
            mean = own[0] / FF
            inverse = lax.rsqrt(own[1] / FF - mean * mean + eps)
            plain = own[2] / FF
            against = inverse * (own[3] / FF - mean * plain)
            hat = (active[c] - mean[:, None]) * inverse[:, None]
            low = rounded(hat * hid_gain + hid_shift)
            slope = 0.5 * (1.0 + erf[c]) + hidden[c] * inv_root_two_pi * jnp.exp(
                -0.5 * hidden[c] * hidden[c]
            )
            grad = inverse[:, None] * (scaled[c] - plain[:, None] - hat * against[:, None])
            grad = rounded(grad * slope)
            hid_gain_grad = hid_gain_grad + jnp.sum(hid_back[c] * hat, 0)
            hid_shift_grad = hid_shift_grad + jnp.sum(hid_back[c], 0)
            up_bias_grad = up_bias_grad + jnp.sum(grad, 0, dtype=f32)
            links.mark(low, grad)
            hid_low.append(low)
            hidden_grad.append(grad)
            if c == chunks - 1:
                down_grad = jnp.einsum(
                    "tf,td->fd", links.then(joined(hid_low)), cot, preferred_element_type=f32
                )
                links.mark(down_grad)
                down_part = lax.psum_scatter(down_grad, "dp", scatter_dimension=1, tiled=True)
            grad = links.then(grad)
            second_grad.append(
                Scatter(
                    links,
                    [
                        jnp.einsum("tf,df->td", grad, up_weight[a:b], preferred_element_type=f32)
                        for a, b, _ in links.halves()
                    ],
                )
            )
        second_grad[0].step()
        up_grad = jnp.einsum(
            "td,tf->df",
            links.then(joined(second)),
            joined(hidden_grad),
            preferred_element_type=f32,
        )
        links.mark(up_grad)
        up_part = lax.psum_scatter(up_grad, "dp", scatter_dimension=0, tiled=True)
        for grad in second_grad[1:]:
            grad.step()

        middle_grad, branch_low, result = [], [], []
        ffn_gain_grad, ffn_shift_grad, out_bias_grad, down_bias_grad = 0.0, 0.0, 0.0, 0.0
        for c in each:
            upstream = own_rows(cotangent, c)
            own = second_grad[c].finish()
            ffn_gain_grad = ffn_gain_grad + jnp.sum(own * ffn_hat[c], 0)
            ffn_shift_grad = ffn_shift_grad + jnp.sum(own, 0)
            grad = upstream + local_back(own, ffn_hat[c], ffn_gain, ffn_inv[c])
            out_bias_grad = out_bias_grad + jnp.sum(grad, 0)
            down_bias_grad = down_bias_grad + jnp.sum(upstream, 0)
            middle_grad.append(grad)
            branch_low.append(Gather(links, grad))
            low = links.then(hid_low[c])
            parts = [matmul(low, w) for w in columns(down_weight)]
            links.mark(parts)
            result.append(parts)
            branch_low[c].step()
        mix_gain_grad, mix_shift_grad, qkv_bias_grad = 0.0, 0.0, 0.0
        proj_grad, first_grad, sums, mix_scaled = [], [], [], []
        for c in each:
            branch_low[c] = assembled(branch_low[c].result())
            result[c] = Scatter(links, result[c])
            back = jnp.einsum("td,ed->te", branch_low[c], out_weight, preferred_element_type=f32)
            mix_gain_grad = mix_gain_grad + jnp.sum(back * mix_hat[c], 0)
            mix_shift_grad = mix_shift_grad + jnp.sum(back, 0)
            mix_scaled.append(back * mix_gain)
            own = jnp.stack([jnp.sum(mix_scaled[c], 1), jnp.sum(mix_scaled[c] * mix_hat[c], 1)])
            links.mark(own)
            sums.append(links.exchange(own))
        out_grad = jnp.einsum(
            "te,td->ed",
            joined(mix_low),
            links.then(joined(branch_low)),
            preferred_element_type=f32,
        )
        links.mark(out_grad)
        out_part = lax.psum_scatter(out_grad, "dp", scatter_dimension=1, tiled=True)
        for c in each:
            own = links.summed(links.then(sums[c]))
            grad = mix_inv[c][:, None] * (
                mix_scaled[c] - own[0][:, None] / D - mix_hat[c] * own[1][:, None] / D
            )
            grads = attend_back(tensor_at, lengths, qkv[c], rounded(grad), tabs, n, c)
            proj_grad.append(grads)
            qkv_bias_grad = qkv_bias_grad + jnp.sum(grads, 1, dtype=f32)
            first_grad.append(
                Scatter(
                    links,
                    [
                        jnp.einsum(
                            "cte,cde->td", grads, qkv_weight[:, a:b], preferred_element_type=f32
                        )
                        for a, b, _ in links.halves()
                    ],
                )
            )
        qkv_grad = jnp.einsum(
            "td,cte->cde",
            joined(first),
            links.then(joined(proj_grad)),
            preferred_element_type=f32,
        )
        links.mark(qkv_grad)
        qkv_part = lax.psum_scatter(qkv_grad, "dp", scatter_dimension=1, tiled=True)

        for c in each:
            result[c].step()
        for c in each:
            first_grad[c].step()
        outputs, grads = [], []
        pre_gain_grad, pre_shift_grad = 0.0, 0.0
        for c in each:
            outputs.append(Gather(links, middle[c] + result[c].finish() + down_bias))
        for c in each:
            hat, inverse = local_norm(own_rows(tokens, c))
            own = first_grad[c].finish()
            pre_gain_grad = pre_gain_grad + jnp.sum(own * hat, 0)
            pre_shift_grad = pre_shift_grad + jnp.sum(own, 0)
            grads.append(Gather(links, middle_grad[c] + local_back(own, hat, pre_gain, inverse)))
        for c in each:
            outputs[c].step()
        for c in each:
            grads[c].step()
        output, tokens_grad = None, None
        for c in each:
            output = placed(tensor_at, outputs[c].result(), c, chunks, bf16, output)
        for c in each:
            tokens_grad = placed(tensor_at, grads[c].result(), c, chunks, f32, tokens_grad)

        whole = links.spread(
            jnp.concatenate([ffn_gain_grad, ffn_shift_grad, out_bias_grad, down_bias_grad]),
            "tensor",
        )
        parts = [
            whole,
            up_bias_grad,
            hid_gain_grad,
            hid_shift_grad,
            mix_gain_grad,
            mix_shift_grad,
        ]
        early = links.spread(jnp.concatenate(parts), "dp")
        early = jnp.split(early, np.cumsum([D, D, D] + [p.shape[0] for p in [whole[:D]] + parts[1:-1]]))
        whole = links.spread(jnp.concatenate([pre_gain_grad, pre_shift_grad]), "tensor")
        late = links.spread(jnp.concatenate([whole, qkv_bias_grad.reshape(-1)]), "dp")
        return (
            output.reshape(tokens.shape),
            tokens_grad.reshape(tokens.shape),
            late[:D],
            late[D : 2 * D],
            qkv_part,
            late[2 * D :].reshape(qkv_bias.shape),
            early[7],
            early[8],
            out_part,
            early[2],
            early[0],
            early[1],
            up_part,
            early[4],
            early[5],
            early[6],
            down_part,
            early[3],
        )

    return body


def solution(mesh):
    in_specs = (
        P("dp", None),
        P("dp"),
        P("dp", None),
        P(),
        P(),
        P(None, None, "tensor"),
        P(None, "tensor"),
        P("tensor"),
        P("tensor"),
        P("tensor", None),
        P(),
        P(),
        P(),
        P(None, "tensor"),
        P("tensor"),
        P("tensor"),
        P("tensor"),
        P("tensor", None),
        P(),
    )
    out_specs = (
        P("dp", None),
        P("dp", None),
        P(),
        P(),
        P(None, "dp", "tensor"),
        P(None, "tensor"),
        P("tensor"),
        P("tensor"),
        P("tensor", "dp"),
        P(),
        P(),
        P(),
        P("dp", "tensor"),
        P("tensor"),
        P("tensor"),
        P("tensor"),
        P("tensor", "dp"),
        P(),
    )
    body = make_body(mesh.shape["tensor"], mesh.shape["dp"])
    return jax.shard_map(body, mesh=mesh, in_specs=in_specs, out_specs=out_specs, check_vma=False)
```
